32 devices in a mesh: dp: 8 (over y, x, core), tensor: 4 (over z).
Axes of the slice: x: 2, y: 2, z: 4, core: 2. Of those that a mesh axis runs over, the one named last changes fastest.
Arguments:
- tokens: bfloat16 [16384, 768], P(('dp', 'tensor')), may hold values from -6 to 6
- qkv_weight: bfloat16 [3, 768, 768], P(None, None, 'tensor'), may hold values from -0.21875 to 0.21875
- rel_weight: bfloat16 [768, 64], P('tensor'), may hold values from -0.75 to 0.75
- out_weight: bfloat16 [768, 768], P('tensor'), may hold values from -1.75 to 1.75
- ffn_in_weight: bfloat16 [768, 3072], P(None, 'tensor'), may hold values from -0.21875 to 0.21875
- ffn_in_bias: float32 [3072], P('tensor'), may hold values from -3 to 3
- ffn_out_weight: bfloat16 [3072, 768], P('tensor'), may hold values from -0.109375 to 0.109375
- norm_gains: float32 [2, 768], replicated, may hold values from 0.5 to 1.5
- norm_biases: float32 [2, 768], replicated, may hold values from -3 to 3
- page_lengths: int32 [32], P('dp'), may hold values from 40 to 512, as said below
- boxes: int32 [2, 16384], P(None, 'dp'), may hold values from 0 to 1000
- out_grad: bfloat16 [16384, 768], P(('dp', 'tensor')), may hold values from -6 to 6
Outputs:
- layer_out: bfloat16 [16384, 768], P(('dp', 'tensor'))
- tokens_grad: bfloat16 [16384, 768], P(('dp', 'tensor'))
- qkv_grad: float32 [3, 768, 768], P(None, None, 'tensor')
- rel_grad: float32 [768, 64], P('tensor')
- out_weight_grad: float32 [768, 768], P('tensor')
- ffn_in_grad: float32 [768, 3072], P(None, 'tensor')
- ffn_bias_grad: float32 [3072], P('tensor')
- ffn_out_grad: float32 [3072, 768], P('tensor')
- gains_grad: float32 [2, 768], replicated
- biases_grad: float32 [2, 768], replicated
- masked_rms: float32 [3], replicated
The draws below stay inside these ranges and needn't reach their ends.
Inputs may be any that keep to these rules, and one draw needn't show every extreme that they name: `page_lengths`: lengths of 40 and of 512 occur in every draw.
All inputs are finite; a program needn't handle non-finite values.
Results may differ from the reference program's by a relative error of at most 0.018.
Values may be sent and summed in bfloat16 or wider, within the bound.
A program may use at most 128 MiB of HBM per device.

```python
import math
import jax
import jax.numpy as jnp
from jax import lax

D = 768
HEADS = 12
HEAD_DIM = 64
FF = 3072
PAGE = 512
PAGES_DEV = 4
FREQ = 16
POS = 64
HD = 768
PAGES = 32
TOKENS = 16384


def draw_page_lengths(key, part):
    raw_lengths = jax.random.randint(key, (PAGES,), 40, PAGE + 1)
    places = jnp.arange(PAGES)
    return jnp.where(places == 0, PAGE, jnp.where(places == 1, 40, raw_lengths)).astype(jnp.int32)


def place_ends(entries, rng, low, high):
    spot = [jax.random.randint(jax.random.fold_in(rng, axis), (), 0, length) for axis, length in enumerate(entries.shape)]
    main_axis = entries.shape.index(max(entries.shape))
    next_to = spot[:main_axis] + [(spot[main_axis] + 1) % entries.shape[main_axis]] + spot[main_axis + 1:]
    return entries.at[tuple(spot)].set(low).at[tuple(next_to)].set(high)


def block_levels(key, dims, pieces, least, top_value):
    loudness, own = 1.0, jax.random.fold_in(key, 6)
    for position, shards_of in pieces:
        steps = jnp.exp(jax.random.uniform(jax.random.fold_in(own, position), (shards_of,), jnp.float32, least / len(pieces), top_value / len(pieces)))
        loudness = loudness * jnp.repeat(steps, dims[position] // shards_of).reshape([-1 if axis == position else 1 for axis in range(len(dims))])
    return loudness


def normal_values(stream_key, extent, scale, most, cuts=(), held_as=jnp.bfloat16):
    values = jax.random.normal(stream_key, extent, jnp.float32) * scale
    if len(cuts) > 0:
        values = block_levels(stream_key, extent, cuts, -0.22, 0.18) * values
    return jnp.clip(values, min=-most, max=most).astype(held_as)


def setup_inputs(seed: int = 0) -> dict:
    seeds = jax.random.split(jax.random.key(seed), 13)
    tokens = normal_values(seeds[0], (TOKENS, D), 1.0, 6.0, ((0, 32),))
    qkv_weight = normal_values(seeds[1], (3, D, HD), D ** -0.5, 0.21875, ((2, 4),))
    rel_weight = normal_values(seeds[2], (HD, POS), HEAD_DIM ** -0.5, 0.75, ((0, 4),))
    out_weight = normal_values(seeds[3], (HD, D), HEADS ** -0.5, 1.75, ((0, 4),))
    ffn_in_weight = normal_values(seeds[4], (D, FF), D ** -0.5, 0.21875, ((1, 4),))
    ffn_in_bias = normal_values(seeds[5], (FF,), 0.5, 3.0, ((0, 4),), jnp.float32)
    ffn_out_weight = normal_values(seeds[6], (FF, D), FF ** -0.5, 0.109375, ((0, 4),))
    norm_gains = jnp.clip(1.0 + 0.1 * jax.random.normal(seeds[7], (2, D), jnp.float32), 0.5, 1.5)
    norm_biases = normal_values(seeds[8], (2, D), 0.5, 3.0, (), jnp.float32)
    page_lengths = draw_page_lengths(jax.random.fold_in(seeds[12], 71), 0)
    boxes = place_ends(jax.random.randint(seeds[10], (2, TOKENS), 0, 1001), jax.random.fold_in(seeds[10], 1), 0, 1000).astype(jnp.int32)
    out_grad = normal_values(seeds[11], (TOKENS, D), 1.0, 6.0, ((0, 32),))
    return dict(tokens=tokens, qkv_weight=qkv_weight, rel_weight=rel_weight, out_weight=out_weight, ffn_in_weight=ffn_in_weight, ffn_in_bias=ffn_in_bias, ffn_out_weight=ffn_out_weight, norm_gains=norm_gains, norm_biases=norm_biases, page_lengths=page_lengths, boxes=boxes, out_grad=out_grad)


@jax.custom_vjp
def low(v):
    return lax.optimization_barrier(v.astype(jnp.bfloat16)).astype(jnp.float32)

@jax.custom_vjp
def low_back(v):
    return v

def low_keep(v):
    return (low(v), None)

def low_pass(kept, grad):
    return (grad,)

def back_keep(v):
    return (v, None)

def back_low(kept, grad):
    return (low(grad),)
low.defvjp(low_keep, low_pass)
low_back.defvjp(back_keep, back_low)
highest = lax.Precision.HIGHEST
norm_epsilon = 1e-05
score_scale = 0.125
masked_score = -1000000000.0

def position_features(boxes_rows):
    orders = jnp.arange(FREQ, dtype=jnp.float32)
    rates = 0.5 * jnp.exp(orders * (-math.log(100.0) / FREQ))
    angles = boxes_rows.astype(jnp.float32)[:, None, :] * rates[None, :, None]
    angles = angles.reshape(2 * FREQ, boxes_rows.shape[1])
    return jnp.concatenate([jnp.cos(angles), jnp.sin(angles)], 0).T

def rotate(coeffs, cos_part, sin_part):
    halfway = coeffs.shape[-1] // 2
    first, second = (coeffs[..., :halfway], coeffs[..., halfway:])
    return jnp.concatenate([first * sin_part + second * cos_part, second * sin_part - first * cos_part], -1)

def layer_norm(values, gain, shift):
    average = lax.optimization_barrier(jnp.mean(values, -1, keepdims=True))
    centred = values - average
    spread = lax.optimization_barrier(jnp.mean(centred * centred, -1, keepdims=True))
    return centred * lax.rsqrt(spread + norm_epsilon) * gain + shift

def attend(member):
    queries_page, keys_page, values_page, key_valid = member
    scores = low_back(jnp.einsum('qhe,khe->hqk', queries_page, keys_page, precision=highest) * score_scale)
    scores = jnp.where(key_valid[None, None, :], scores, masked_score)
    weights = low(jax.nn.softmax(scores, axis=-1))
    return jnp.einsum('hqk,khd->qhd', weights, values_page, precision=highest)

def forward_group(tokens_rows, qkv_weight, rel_weight, out_weight, ffn_in_weight, ffn_in_bias, ffn_out_weight, norm_gains, norm_biases, features, key_valid):
    count_rows = tokens_rows.shape[0]
    projected = low(low_back(jnp.einsum('td,cdh->cth', tokens_rows, qkv_weight, precision=highest)))
    queries = projected[0].reshape(count_rows, HEADS, HEAD_DIM)
    keys_head = projected[1].reshape(count_rows, HEADS, HEAD_DIM)
    values_head = projected[2].reshape(count_rows, HEADS, HEAD_DIM)
    relation = rel_weight.reshape(HEADS, HEAD_DIM, POS)
    coeffs = low_back(jnp.einsum('thd,hdp->thp', queries, relation, precision=highest))
    halfway = POS // 2
    cos_part = features[:, None, :halfway]
    sin_part = features[:, None, halfway:]
    turned = low(low_back(rotate(coeffs, cos_part, sin_part)))
    placed = jnp.broadcast_to(low(features)[:, None, :], (count_rows, HEADS, POS))
    query_full = jnp.concatenate([queries, turned], -1)
    key_full = jnp.concatenate([keys_head, placed], -1)

    def to_pages(array):
        return array.reshape((key_valid.shape[0], PAGE) + array.shape[1:])
    attended = lax.map(jax.checkpoint(attend), (to_pages(query_full), to_pages(key_full), to_pages(values_head), key_valid))
    attended = low(low_back(attended.reshape(count_rows, HD)))
    attn_out = low_back(jnp.dot(attended, out_weight, precision=highest))
    normed = layer_norm(tokens_rows + attn_out, norm_gains[0], norm_biases[0])
    hidden_pre = low_back(jnp.dot(low(normed), ffn_in_weight, precision=highest) + ffn_in_bias)
    hidden = low(jax.nn.gelu(hidden_pre, approximate=False))
    ffn_out = low_back(jnp.dot(hidden, ffn_out_weight, precision=highest))
    result = layer_norm(normed + ffn_out, norm_gains[1], norm_biases[1])
    return (result, (attn_out, ffn_out))

def reference(tokens, qkv_weight, rel_weight, out_weight, ffn_in_weight, ffn_in_bias, ffn_out_weight, norm_gains, norm_biases, page_lengths, boxes, out_grad):
    weights_all = tuple((member.astype(jnp.float32) for member in (qkv_weight, rel_weight, out_weight, ffn_in_weight, ffn_in_bias, ffn_out_weight, norm_gains, norm_biases)))
    groups = PAGES // PAGES_DEV
    group_rows = PAGES_DEV * PAGE
    inputs = (tokens.reshape(groups, group_rows, D), out_grad.reshape(groups, group_rows, D), page_lengths.reshape(groups, PAGES_DEV), jnp.transpose(boxes.reshape(2, groups, group_rows), (1, 0, 2)))

    def group_step(carry, member):
        totals, square_sums = carry
        rows_in, rows_grad, lengths_group, boxes_group = member
        features = position_features(boxes_group)
        key_valid = jnp.arange(PAGE, dtype=jnp.int32)[None, :] < lengths_group[:, None]

        def forward(rows_value, *params):
            return forward_group(rows_value, *params, features, key_valid)
        rows_value = rows_in.astype(jnp.float32)
        result, backward, extras = jax.vjp(forward, rows_value, *weights_all, has_aux=True)
        gradients = backward(rows_grad.astype(jnp.float32))
        totals = tuple((running + fresh for running, fresh in zip(totals, gradients[1:])))
        valid_rows = key_valid.reshape(group_rows, 1).astype(jnp.float32)
        attn_out, ffn_out = extras
        squares = jnp.stack([jnp.sum(valid_rows * rows_value * rows_value), jnp.sum(valid_rows * attn_out * attn_out), jnp.sum(valid_rows * ffn_out * ffn_out), jnp.sum(valid_rows) * D])
        return ((totals, square_sums + squares), (result.astype(jnp.bfloat16), gradients[0].astype(jnp.bfloat16)))
    initial = (tuple((jnp.zeros_like(member) for member in weights_all)), jnp.zeros((4,), jnp.float32))
    (totals, square_sums), (outputs, input_grads) = lax.scan(group_step, initial, inputs)
    root_means = jnp.sqrt(square_sums[:3] / square_sums[3])
    return (outputs.reshape(TOKENS, D), input_grads.reshape(TOKENS, D), totals[0], totals[1], totals[2], totals[3], totals[4], totals[5], totals[6], totals[7], root_means)
```

```python
from functools import partial
import math

import jax
import jax.numpy as jnp
from jax import lax
from jax.experimental import pallas as pl
from jax.experimental.pallas import tpu as pltpu
from jax.sharding import PartitionSpec as P

HEAD_DIM = 64
PAGE = 512
FREQ = 16
POS = 64
SPLIT = 8

norm_epsilon = 1e-05
score_scale = 0.125
masked_score = -1000000000.0

bf16 = jnp.bfloat16
f32 = jnp.float32


def position_features(boxes_rows):
    orders = jnp.arange(FREQ, dtype=jnp.float32)
    rates = 0.5 * jnp.exp(orders * (-math.log(100.0) / FREQ))
    angles = boxes_rows.astype(jnp.float32)[:, None, :] * rates[None, :, None]
    angles = angles.reshape(2 * FREQ, boxes_rows.shape[1])
    return jnp.concatenate([jnp.cos(angles), jnp.sin(angles)], 0).T


def rotate(coeffs, cos_part, sin_part):
    halfway = coeffs.shape[-1] // 2
    first, second = (coeffs[..., :halfway], coeffs[..., halfway:])
    return jnp.concatenate(
        [first * sin_part + second * cos_part, second * sin_part - first * cos_part], -1
    )


def rotate_back(grad_turned, cos_part, sin_part):
    halfway = grad_turned.shape[-1] // 2
    first, second = (grad_turned[..., :halfway], grad_turned[..., halfway:])
    return jnp.concatenate(
        [first * sin_part - second * cos_part, first * cos_part + second * sin_part], -1
    )


def layer_norm(values, gain, shift):
    average = jnp.mean(values, -1, keepdims=True)
    centred = values - average
    spread = jnp.mean(centred * centred, -1, keepdims=True)
    return centred * lax.rsqrt(spread + norm_epsilon) * gain + shift


class Place:
    def __init__(self, dp_size):
        d = lax.axis_index("dp")
        t = lax.axis_index("tensor")
        sub = d % SPLIT
        c = sub % 2
        x = (sub // 2) % 2
        y = sub // 4
        self.d, self.t, self.c = d, t, c
        self.tk = (t, t + 1 - 2 * (t % 2), t + 2 - 4 * (t // 2), 3 - t)
        step_x = (1 - 2 * x) * 2
        step_y = (1 - 2 * y) * 4
        step_1 = (1 - c) * step_x + c * step_y
        step_2 = c * step_x + (1 - c) * step_y
        self.dev_c = d + 1 - 2 * c
        self.dev_1 = d + step_1
        self.dev_2 = d + step_2
        self.yx = sub // 2
        self.yx_1 = (sub + step_1) // 2
        self.yx_2 = (sub + step_2) // 2
        self.yx_12 = (sub + step_1 + step_2) // 2
        self.far = []
        width = SPLIT
        while width < dp_size:
            self.far.append(d + width * (1 - 2 * ((d // width) % 2)))
            width *= 2


def meet(place):
    barrier = pltpu.get_barrier_semaphore()
    targets = [{"dp": v} for v in (place.dev_c, place.dev_1, place.dev_2, *place.far)]
    targets += [{"tensor": place.tk[1]}, {"tensor": place.tk[2]}]
    for target in targets:
        pl.semaphore_signal(barrier, inc=1, device_id=target, device_id_type=pl.DeviceIdType.MESH)
    pl.semaphore_wait(barrier, len(targets))


def remote(source, target, sems, index, device):
    send, recv = sems
    return pltpu.make_async_remote_copy(
        src_ref=source,
        dst_ref=target,
        send_sem=send.at[index],
        recv_sem=recv.at[index],
        device_id=device,
        device_id_type=pl.DeviceIdType.MESH,
    )


def gather_kernel(dp_size, *refs):
    own = refs[0:3]
    rel_own, bias_own = refs[3:5]
    whole = refs[5:8]
    rel_all, bias_all = refs[8:10]
    local_sem, z_send, z_recv, p_send, p_recv, s_send, s_recv = refs[10:]
    zs, ps, ss = (z_send, z_recv), (p_send, p_recv), (s_send, s_recv)
    here = Place(dp_size)
    t, c, yx = here.t, here.c, here.yx
    rows = own[0].shape[2]
    local = []
    for a in range(3):
        local.append(pltpu.make_async_copy(own[a], whole[a].at[t], local_sem.at[a]))
    local.append(pltpu.make_async_copy(rel_own, rel_all.at[t], local_sem.at[3]))
    local.append(pltpu.make_async_copy(bias_own, bias_all.at[t], local_sem.at[4]))
    for copy in local:
        copy.start()
    meet(here)
    t1, t2 = {"tensor": here.tk[1]}, {"tensor": here.tk[2]}
    started = []

    def go(copy):
        copy.start()
        started.append(copy)
        return copy

    small = []
    for i, (mine, every) in enumerate(((rel_own, rel_all), (bias_own, bias_all))):
        small.append(
            (
                go(remote(mine, every.at[t], ss, (i, 0), t1)),
                go(remote(mine, every.at[t], ss, (i, 1), t2)),
            )
        )
    along = []
    for a in range(3):
        piece = own[a].at[yx, c]
        spot = whole[a].at[t, yx, c]
        along.append(
            [go(remote(piece, spot, zs, (a, 0), t1)), go(remote(piece, spot, zs, (a, 1), t2))]
        )
    for i, every in enumerate((rel_all, bias_all)):
        small[i][0].wait_recv()
        spot = every.at[here.tk[1]]
        small[i] = small[i] + (go(remote(spot, spot, ss, (i, 2), t2)),)

    def plane_one(a, k):
        spot = whole[a].at[here.tk[k], yx, c]
        return [go(remote(spot, spot, ps, (a, k, 0), {"dp": here.dev_1}))]

    def plane_two(a, k):
        out = []
        for i, place in enumerate((yx, here.yx_1)):
            spot = whole[a].at[here.tk[k], place, c]
            out.append(go(remote(spot, spot, ps, (a, k, 1 + i), {"dp": here.dev_2})))
        return out

    def plane_three(a, k):
        spot = whole[a].at[here.tk[k], :, c]
        return [go(remote(spot, spot, ps, (a, k, 3), {"dp": here.dev_c}))]

    units = [(a, k) for a in range(3) for k in (1, 2, 3)]
    flight = {}
    for i in range(len(units) + 3):
        if i < len(units):
            a, k = units[i]
            along[a][k - 1].wait_recv()
            if k == 1:
                spot = whole[a].at[here.tk[1], yx, c]
                along[a].append(go(remote(spot, spot, zs, (a, 2), t2)))
            flight[a, k, 1] = plane_one(a, k)
        for lag, step in ((1, plane_two), (2, plane_three)):
            if 0 <= i - lag < len(units):
                a, k = units[i - lag]
                for copy in flight[a, k, lag]:
                    copy.wait_recv()
                flight[a, k, lag + 1] = step(a, k)
        if 0 <= i - 3 < len(units):
            a, k = units[i - 3]
            for copy in flight[a, k, 3]:
                copy.wait_recv()
    for i in range(2):
        small[i][1].wait_recv()
        small[i][2].wait_recv()
    for copy in started:
        copy.wait_send()
    for copy in local:
        copy.wait()


def gather_weights(dp_size, own, rel_own, bias_own):
    vmem = pl.BlockSpec(memory_space=pltpu.VMEM)
    anywhere = pl.BlockSpec(memory_space=pl.ANY)
    shapes = [jax.ShapeDtypeStruct((4,) + a.shape, a.dtype) for a in (*own, rel_own, bias_own)]
    dma = pltpu.SemaphoreType.DMA
    return pl.pallas_call(
        partial(gather_kernel, dp_size),
        out_shape=shapes,
        in_specs=[anywhere] * 5,
        out_specs=[vmem] * 5,
        scratch_shapes=[
            dma((5,)),
            dma((3, 3)),
            dma((3, 3)),
            dma((3, 4, 4)),
            dma((3, 4, 4)),
            dma((2, 3)),
            dma((2, 3)),
        ],
        compiler_params=pltpu.CompilerParams(
            collective_id=0, has_side_effects=True, vmem_limit_bytes=60 * 1024 * 1024
        ),
        name="gather_weights",
    )(*own, rel_own, bias_own)


def reduce_kernel(dp_size, n_far, *refs):
    grads_in = refs[0:4]
    sums_in = refs[4]
    outs = refs[5:9]
    sums_out = refs[9]
    grads = refs[10:14]
    got_c = refs[14:18]
    got_1 = refs[18:22]
    got_2 = refs[22:26]
    got_z = refs[26:30]
    got_far = refs[30:34]
    sums_tx, sums_rx = refs[34:36]
    local_sem, g_send, g_recv, f_send, f_recv, s_send, s_recv = refs[36:]
    gs, fs, sm = (g_send, g_recv), (f_send, f_recv), (s_send, s_recv)
    here = Place(dp_size)
    c, yx = here.c, here.yx
    arrays = range(4)
    local = {}
    for a in arrays:
        for k in (3, 2, 1, 0):
            copy = pltpu.make_async_copy(
                grads_in[a].at[here.tk[k]], grads[a].at[here.tk[k]], local_sem.at[a, k]
            )
            copy.start()
            local[a, k] = copy
    meet(here)
    started = []

    def go(copy):
        copy.start()
        started.append(copy)
        return copy

    t1, t2 = {"tensor": here.tk[1]}, {"tensor": here.tk[2]}
    butterfly = [{"dp": here.dev_c}, {"dp": here.dev_1}, {"dp": here.dev_2}, t1, t2]
    butterfly += [{"dp": v} for v in here.far]
    sums_tx[0] = sums_in[...]
    flow = {}
    sums_flow = [go(remote(sums_tx.at[0], sums_rx.at[0], sm, (0,), butterfly[0]))]

    def sums_step(i):
        sums_flow[i].wait_recv()
        total = sums_tx[i] + sums_rx[i]
        if i + 1 < len(butterfly):
            sums_tx[i + 1] = total
            sums_flow.append(
                go(remote(sums_tx.at[i + 1], sums_rx.at[i + 1], sm, (i + 1,), butterfly[i + 1]))
            )
        else:
            sums_out[...] = total

    def start_c(a, k):
        local[a, k].wait()
        tk = here.tk[k]
        flow[a, k, 0] = [
            go(
                remote(
                    grads[a].at[tk, :, 1 - c], got_c[a].at[k], gs, (a, k, 0), {"dp": here.dev_c}
                )
            )
        ]

    def take_c(a, k):
        tk = here.tk[k]
        flow[a, k, 0][0].wait_recv()

        def body(i, carry):
            grads[a][tk, i, c] = grads[a][tk, i, c] + got_c[a][k, i]
            return carry

        lax.fori_loop(0, 4, body, 0)
        flow[a, k, 1] = [
            go(
                remote(
                    grads[a].at[tk, here.yx_1, c],
                    got_1[a].at[k, 0],
                    gs,
                    (a, k, 1),
                    {"dp": here.dev_1},
                )
            ),
            go(
                remote(
                    grads[a].at[tk, here.yx_12, c],
                    got_1[a].at[k, 1],
                    gs,
                    (a, k, 2),
                    {"dp": here.dev_1},
                )
            ),
        ]

    def take_1(a, k):
        tk = here.tk[k]
        for copy in flow[a, k, 1]:
            copy.wait_recv()
        grads[a][tk, here.yx_2, c] = grads[a][tk, here.yx_2, c] + got_1[a][k, 1]
        flow[a, k, 2] = [
            go(
                remote(
                    grads[a].at[tk, here.yx_2, c],
                    got_2[a].at[k],
                    gs,
                    (a, k, 3),
                    {"dp": here.dev_2},
                )
            )
        ]
        grads[a][tk, yx, c] = grads[a][tk, yx, c] + got_1[a][k, 0]

    def take_2(a, k):
        tk = here.tk[k]
        flow[a, k, 2][0].wait_recv()
        grads[a][tk, yx, c] = grads[a][tk, yx, c] + got_2[a][k]
        if k >= 2:
            flow[a, k, 3] = [
                go(remote(grads[a].at[tk, yx, c], got_z[a].at[k - 2], gs, (a, k, 4), t2))
            ]
        else:
            flow[a, k + 2, 3][0].wait_recv()
            grads[a][tk, yx, c] = grads[a][tk, yx, c] + got_z[a][k]
            if k == 1:
                flow[a, 1, 3] = [
                    go(remote(grads[a].at[tk, yx, c], got_z[a].at[2], gs, (a, 1, 4), t1))
                ]

    def take_z(a):
        tk = here.tk[0]
        flow[a, 1, 3][0].wait_recv()
        grads[a][tk, yx, c] = grads[a][tk, yx, c] + got_z[a][2]
        for i, v in enumerate(here.far):
            copy = go(remote(grads[a].at[tk, yx, c], got_far[a].at[i], fs, (a, 4 + i), {"dp": v}))
            copy.wait()
            grads[a][tk, yx, c] = grads[a][tk, yx, c] + got_far[a][i]
        outs[a][yx, c] = grads[a][tk, yx, c]
        spot = outs[a].at[yx, c]
        flow[a, 0] = [go(remote(spot, spot, fs, (a, 0), {"dp": here.dev_1}))]

    def back_1(a):
        flow[a, 0][0].wait_recv()
        flow[a, 1] = []
        for i, place in enumerate((yx, here.yx_1)):
            spot = outs[a].at[place, c]
            flow[a, 1].append(go(remote(spot, spot, fs, (a, 1 + i), {"dp": here.dev_2})))

    def back_2(a):
        for copy in flow[a, 1]:
            copy.wait_recv()
        spot = outs[a].at[:, c]
        flow[a, 2] = [go(remote(spot, spot, fs, (a, 3), {"dp": here.dev_c}))]

    def back_3(a):
        flow[a, 2][0].wait_recv()

    units = [(a, k) for a in arrays for k in (3, 2, 1, 0)]
    for a, k in units:
        start_c(a, k)
    for i in range(len(units) + 8):
        if i < len(units):
            take_c(*units[i])
        if 0 <= i - 1 < len(units):
            take_1(*units[i - 1])
        if i < len(butterfly):
            sums_step(i)
        if 0 <= i - 2 < len(units):
            take_2(*units[i - 2])
        for lag, step in ((3, take_z), (4, back_1), (5, back_2), (6, back_3)):
            j = i - lag
            if 0 <= j < len(units) and units[j][1] == 0:
                step(units[j][0])
    for i in range(len(units) + 8, len(butterfly)):
        sums_step(i)
    for copy in started:
        copy.wait_send()


def reduce_grads(dp_size, grads, sums):
    vmem = pl.BlockSpec(memory_space=pltpu.VMEM)
    anywhere = pl.BlockSpec(memory_space=pl.ANY)
    n_far = max(0, (dp_size // SPLIT).bit_length() - 1)
    steps = 5 + n_far
    dma = pltpu.SemaphoreType.DMA
    scratch = []
    pieces = [g.shape[3:] for g in grads]
    types = [g.dtype for g in grads]
    for lead in ((4, 4, 2), (4, 4), (4, 2), (4,), (3,), (max(1, n_far),)):
        scratch += [pltpu.VMEM(lead + p, k) for p, k in zip(pieces, types)]
    scratch += [pltpu.VMEM((steps,) + sums.shape, f32)] * 2
    scratch += [
        dma((4, 4)),
        dma((4, 4, 5)),
        dma((4, 4, 5)),
        dma((4, 4 + max(1, n_far))),
        dma((4, 4 + max(1, n_far))),
        dma((steps,)),
        dma((steps,)),
    ]
    shapes = [jax.ShapeDtypeStruct((4, 2) + p, k) for p, k in zip(pieces, types)]
    shapes.append(jax.ShapeDtypeStruct(sums.shape, f32))
    return pl.pallas_call(
        partial(reduce_kernel, dp_size, n_far),
        out_shape=shapes,
        in_specs=[anywhere] * 4 + [vmem],
        out_specs=[vmem] * 5,
        scratch_shapes=scratch,
        compiler_params=pltpu.CompilerParams(
            collective_id=1, has_side_effects=True, vmem_limit_bytes=60 * 1024 * 1024
        ),
        name="reduce_grads",
    )(*grads, sums)


def per_device(
    dp_size,
    tokens,
    qkv_weight,
    rel_weight,
    out_weight,
    ffn_in_weight,
    ffn_in_bias,
    ffn_out_weight,
    norm_gains,
    norm_biases,
    page_lengths,
    boxes,
    out_grad,
):
    rows, width = tokens.shape
    part = out_weight.shape[0]
    shards = boxes.shape[1] // rows
    heads_part = part // HEAD_DIM
    heads = heads_part * shards
    t = lax.axis_index("tensor")
    boxes_page = lax.dynamic_slice(boxes, (0, t * rows), (2, rows))
    length = lax.dynamic_index_in_dim(page_lengths, t, 0, keepdims=False)
    features = position_features(boxes_page)
    halfway = POS // 2
    cos_part = features[:, None, :halfway]
    sin_part = features[:, None, halfway:]
    key_valid = jnp.arange(rows, dtype=jnp.int32) < length
    valid_rows = key_valid.astype(f32)[:, None]

    attn_own = jnp.concatenate(
        [jnp.transpose(qkv_weight, (0, 2, 1)).reshape(3 * part, width), out_weight], 0
    )
    split = lambda w: w.reshape(4, 2, w.shape[0] // SPLIT, w.shape[1])
    rel_own = jnp.pad(rel_weight, ((0, 0), (0, 128 - POS)))
    attn_all, in_all, out_all, rel_all, bias_all = gather_weights(
        dp_size,
        (split(attn_own), split(ffn_in_weight), split(ffn_out_weight)),
        rel_own,
        ffn_in_bias.reshape(1, -1),
    )
    attn_all = attn_all.reshape(shards, 4 * part, width)
    qkv_all = attn_all[:, : 3 * part].reshape(shards, 3, part, width)
    proj_out = attn_all[:, 3 * part :].reshape(shards * part, width)
    w_in = in_all.reshape(shards, width, -1)
    w_out = out_all.reshape(-1, width)
    relation = rel_all[:, :, :POS].reshape(heads, HEAD_DIM, POS)
    bias = bias_all.reshape(shards, -1)

    projected = jnp.einsum("td,scnd->ctsn", tokens, qkv_all, preferred_element_type=f32).astype(
        bf16
    )
    projected = projected.reshape(3, rows, heads, HEAD_DIM)
    queries, keys_head, values = projected[0], projected[1], projected[2]
    coeffs = jnp.einsum("thd,hdp->thp", queries, relation, preferred_element_type=f32)
    turned = rotate(coeffs, cos_part, sin_part).astype(bf16)
    placed = jnp.broadcast_to(features.astype(bf16)[:, None, :], (rows, heads, POS))
    query_full = jnp.concatenate([queries, turned], -1)
    key_full = jnp.concatenate([keys_head, placed], -1)
    scores = (
        jnp.einsum("qhe,khe->hqk", query_full, key_full, preferred_element_type=f32) * score_scale
    )
    scores = jnp.where(key_valid[None, None, :], scores, masked_score)
    raised = jnp.exp(scores - jnp.max(scores, -1, keepdims=True))
    probs = raised / jnp.sum(raised, -1, keepdims=True)
    weights = probs.astype(bf16)
    attended = (
        jnp.einsum("hqk,khd->qhd", weights, values, preferred_element_type=f32)
        .astype(bf16)
        .reshape(rows, heads * HEAD_DIM)
    )
    attn_out = jnp.dot(attended, proj_out, preferred_element_type=f32)
    tokens_value = tokens.astype(f32)
    normed, norm_back_one = jax.vjp(
        layer_norm, tokens_value + attn_out, norm_gains[0], norm_biases[0]
    )
    normed_low = normed.astype(bf16)
    hidden_pre = (
        jnp.einsum("td,sdf->tsf", normed_low, w_in, preferred_element_type=f32) + bias[None]
    ).reshape(rows, -1)
    hidden_act, gelu_back = jax.vjp(partial(jax.nn.gelu, approximate=False), hidden_pre)
    hidden_low = hidden_act.astype(bf16)
    ffn_out = jnp.dot(hidden_low, w_out, preferred_element_type=f32)
    result, norm_back_two = jax.vjp(layer_norm, normed + ffn_out, norm_gains[1], norm_biases[1])
    stats = jnp.stack(
        [
            jnp.sum(valid_rows * tokens_value * tokens_value),
            jnp.sum(valid_rows * attn_out * attn_out),
            jnp.sum(valid_rows * ffn_out * ffn_out),
            jnp.sum(valid_rows) * width,
        ]
    )
    grad_two, gain_two, shift_two = norm_back_two(out_grad.astype(f32))
    grad_ffn = grad_two.astype(bf16)
    ffn_out_grad = jnp.einsum("tf,td->fd", hidden_low, grad_ffn, preferred_element_type=f32)
    grad_hidden = jnp.einsum("td,fd->tf", grad_ffn, w_out, preferred_element_type=f32)
    grad_pre = gelu_back(grad_hidden)[0].astype(bf16)
    ffn_bias_grad = jnp.sum(grad_pre.astype(f32), 0)
    grad_pre_parts = grad_pre.reshape(rows, shards, -1)
    ffn_in_grad = jnp.einsum("td,tsf->sdf", normed_low, grad_pre_parts, preferred_element_type=f32)
    grad_normed = grad_two + jnp.einsum(
        "tsf,sdf->td", grad_pre_parts, w_in, preferred_element_type=f32
    )
    grad_one, gain_one, shift_one = norm_back_one(grad_normed)
    grad_one_low = grad_one.astype(bf16)
    out_weight_grad = jnp.einsum("th,td->hd", attended, grad_one_low, preferred_element_type=f32)
    grad_attended = (
        jnp.einsum("td,hd->th", grad_one_low, proj_out, preferred_element_type=f32)
        .astype(bf16)
        .reshape(rows, heads, HEAD_DIM)
    )
    grad_weights = jnp.einsum("qhd,khd->hqk", grad_attended, values, preferred_element_type=f32)
    inner = jnp.sum(probs * grad_weights, -1, keepdims=True)
    grad_scores = (probs * (grad_weights - inner)).astype(bf16)
    grad_query_full = (
        jnp.einsum("hqk,khe->qhe", grad_scores, key_full, preferred_element_type=f32) * score_scale
    )
    grad_keys = (
        jnp.einsum("hqk,qhe->khe", grad_scores, queries, preferred_element_type=f32) * score_scale
    ).astype(bf16)
    grad_values = jnp.einsum(
        "hqk,qhd->khd", weights, grad_attended, preferred_element_type=f32
    ).astype(bf16)
    grad_turned = grad_query_full[..., HEAD_DIM:].astype(bf16)
    grad_coeffs = rotate_back(grad_turned.astype(f32), cos_part, sin_part).astype(bf16)
    grad_queries = (
        grad_query_full[..., :HEAD_DIM]
        + jnp.einsum("thp,hdp->thd", grad_coeffs, relation, preferred_element_type=f32)
    ).astype(bf16)
    rel_grad = jnp.einsum("thd,thp->hdp", queries, grad_coeffs, preferred_element_type=f32)
    grad_projected = jnp.stack([grad_queries, grad_keys, grad_values]).reshape(
        3, rows, shards, part
    )
    qkv_grad = jnp.einsum("td,ctsn->scnd", tokens, grad_projected, preferred_element_type=f32)
    tokens_grad = (
        grad_one
        + jnp.einsum("ctsn,scnd->td", grad_projected, qkv_all, preferred_element_type=f32)
    ).astype(bf16)

    attn_grad = jnp.concatenate(
        [
            qkv_grad.reshape(shards, 3 * part, width),
            out_weight_grad.reshape(shards, part, width),
        ],
        1,
    ).astype(bf16)
    split4 = lambda g: g.reshape(shards, 4, 2, g.shape[1] // SPLIT, g.shape[2])
    rel_parts = rel_grad.reshape(shards, heads_part, HEAD_DIM, POS)
    rel_parts = jnp.transpose(rel_parts, (0, 2, 1, 3)).reshape(shards, HEAD_DIM, heads_part * POS)
    rel_parts = jnp.pad(rel_parts, ((0, 0), (0, 0), (0, 256 - heads_part * POS)))
    sums = jnp.concatenate(
        [
            jnp.stack([gain_one, gain_two, shift_one, shift_two]),
            ffn_bias_grad.reshape(shards, -1),
            jnp.pad(stats[None], ((0, 0), (0, width - 4))),
            jnp.zeros((16 - 5 - shards, width), f32),
        ],
        0,
    )
    attn_sum, in_sum, out_sum, rel_sum, sums = reduce_grads(
        dp_size,
        (
            split4(attn_grad),
            split4(ffn_in_grad.astype(bf16)),
            split4(ffn_out_grad.astype(bf16).reshape(shards, -1, width)),
            split4(rel_parts),
        ),
        sums,
    )
    attn_sum = attn_sum.reshape(4 * part, width)
    qkv_sum = jnp.transpose(attn_sum[: 3 * part].reshape(3, part, width), (0, 2, 1)).astype(f32)
    rel_out = jnp.transpose(
        rel_sum.reshape(HEAD_DIM, 256)[:, : heads_part * POS].reshape(HEAD_DIM, heads_part, POS),
        (1, 0, 2),
    ).reshape(part, POS)
    bias_out = lax.dynamic_index_in_dim(sums, 4 + t, 0, keepdims=False)
    stats_total = sums[4 + shards]
    return (
        result.astype(bf16),
        tokens_grad,
        qkv_sum,
        rel_out,
        attn_sum[3 * part :].astype(f32),
        in_sum.reshape(width, -1).astype(f32),
        bias_out,
        out_sum.reshape(-1, width).astype(f32),
        sums[0:2],
        sums[2:4],
        jnp.sqrt(stats_total[:3] / stats_total[3]),
    )


def solution(mesh):
    return jax.shard_map(
        partial(per_device, mesh.shape["dp"]),
        mesh=mesh,
        in_specs=(
            P(("dp", "tensor"), None),
            P(None, None, "tensor"),
            P("tensor", None),
            P("tensor", None),
            P(None, "tensor"),
            P("tensor"),
            P("tensor", None),
            P(),
            P(),
            P("dp"),
            P(None, "dp"),
            P(("dp", "tensor"), None),
        ),
        out_specs=(
            P(("dp", "tensor"), None),
            P(("dp", "tensor"), None),
            P(None, None, "tensor"),
            P("tensor", None),
            P("tensor", None),
            P(None, "tensor"),
            P("tensor"),
            P("tensor", None),
            P(),
            P(),
            P(),
        ),
        check_vma=False,
    )
```

```python
from functools import partial
import math

import jax
import jax.numpy as jnp
from jax import lax
from jax.experimental import pallas as pl
from jax.experimental.pallas import tpu as pltpu
from jax.sharding import PartitionSpec as P

HEAD_DIM = 64
PAGE = 512
FREQ = 16
POS = 64
SPLIT = 8
ROWS_STEP = 64
FF_STEP = 256
REL_LANES = 256

norm_epsilon = 1e-05
score_scale = 0.125
masked_score = -1000000000.0

bf16 = jnp.bfloat16
f32 = jnp.float32
MESH = pl.DeviceIdType.MESH


class Place:
    def __init__(self, dp_size):
        d = lax.axis_index("dp")
        t = lax.axis_index("tensor")
        sub = d % SPLIT
        c = sub % 2
        x = (sub // 2) % 2
        y = sub // 4
        self.t, self.c = t, c
        self.shard = (t, t + 1 - 2 * (t % 2), t + 2 - 4 * (t // 2), 3 - t)
        step_x = (1 - 2 * x) * 2
        step_y = (1 - 2 * y) * 4
        step_1 = (1 - c) * step_x + c * step_y
        step_2 = c * step_x + (1 - c) * step_y
        self.core = {"dp": d + 1 - 2 * c}
        self.one = {"dp": d + step_1}
        self.two = {"dp": d + step_2}
        self.near_z = {"tensor": self.shard[1]}
        self.far_z = {"tensor": self.shard[2]}
        self.yx = sub // 2
        self.yx_1 = (sub + step_1) // 2
        self.yx_2 = (sub + step_2) // 2
        self.yx_12 = (sub + step_1 + step_2) // 2
        self.wide = []
        width = SPLIT
        while width < dp_size:
            self.wide.append({"dp": d + width * (1 - 2 * ((d // width) % 2))})
            width *= 2

    def meet(self):
        barrier = pltpu.get_barrier_semaphore()
        others = [self.core, self.one, self.two, self.near_z, self.far_z, *self.wide]
        for other in others:
            pl.semaphore_signal(barrier, inc=1, device_id=other, device_id_type=MESH)
        pl.semaphore_wait(barrier, len(others))


class Sender:
    def __init__(self):
        self.started = []

    def go(self, source, target, sems, index, device):
        send, recv = sems
        copy = pltpu.make_async_remote_copy(
            src_ref=source,
            dst_ref=target,
            send_sem=send.at[index],
            recv_sem=recv.at[index],
            device_id=device,
            device_id_type=MESH,
        )
        copy.start()
        self.started.append(copy)
        return copy

    def drain(self):
        for copy in self.started:
            copy.wait_send()
        self.started = []


def arrived(copies):
    for copy in copies:
        copy.wait_recv()


class Gather:
    def __init__(self, here, sender, whole, sems, rows):
        self.here, self.sender, self.whole = here, sender, whole
        self.z_sems, self.p_sems = sems
        self.rows = rows
        self.flow = {}

    def spot(self, a, k, yx, c):
        start = pl.multiple_of((yx * 2 + c) * self.rows, self.rows)
        return self.whole[a].at[self.here.shard[k], pl.ds(start, self.rows), :]

    def z_start(self, a):
        here = self.here
        mine = self.spot(a, 0, here.yx, here.c)
        self.flow[a, 1, "z"] = self.sender.go(mine, mine, self.z_sems, (a, 0), here.near_z)
        self.flow[a, 2, "z"] = self.sender.go(mine, mine, self.z_sems, (a, 1), here.far_z)

    def z_relay(self, a):
        here = self.here
        self.flow[a, 1, "z"].wait_recv()
        spot = self.spot(a, 1, here.yx, here.c)
        self.flow[a, 3, "z"] = self.sender.go(spot, spot, self.z_sems, (a, 2), here.far_z)

    def one(self, a, k):
        here = self.here
        if k > 1:
            self.flow[a, k, "z"].wait_recv()
        spot = self.spot(a, k, here.yx, here.c)
        self.flow[a, k, 1] = [self.sender.go(spot, spot, self.p_sems, (a, k, 0), here.one)]

    def two(self, a, k):
        here = self.here
        arrived(self.flow[a, k, 1])
        out = []
        for i, yx in enumerate((here.yx, here.yx_1)):
            spot = self.spot(a, k, yx, here.c)
            out.append(self.sender.go(spot, spot, self.p_sems, (a, k, 1 + i), here.two))
        self.flow[a, k, 2] = out

    def three(self, a, k):
        here = self.here
        arrived(self.flow[a, k, 2])
        out = []
        for i in range(4):
            spot = self.spot(a, k, i, here.c)
            out.append(self.sender.go(spot, spot, self.p_sems, (a, k, 3 + i), here.core))
        self.flow[a, k, 3] = out

    def ready(self, a, k):
        arrived(self.flow[a, k, 3])


class Reduce:
    def __init__(self, here, sender, grads, outs, got, sems, rows):
        self.here, self.sender, self.grads, self.outs = here, sender, grads, outs
        self.got_c, self.got_1, self.got_2, self.got_z, self.got_w = got
        self.g_sems, self.o_sems = sems
        self.rows = rows
        self.flow = {}

    def piece(self, a, yx, c):
        rows = self.rows[a]
        return pl.ds(pl.multiple_of((yx * 2 + c) * rows, rows), rows)

    def spot(self, a, k, yx, c):
        return self.grads[a].at[self.here.shard[k], self.piece(a, yx, c), :]

    def add(self, a, k, yx, other):
        here = self.here
        r = self.piece(a, yx, here.c)
        s = here.shard[k]
        self.grads[a][s, r, :] = self.grads[a][s, r, :] + other

    def c_send(self, a, k):
        here = self.here
        self.flow[a, k, 0] = [
            self.sender.go(
                self.spot(a, k, i, 1 - here.c),
                self.got_c[a].at[k, i],
                self.g_sems,
                (a, k, i),
                here.core,
            )
            for i in range(4)
        ]

    def c_take(self, a, k):
        here = self.here
        arrived(self.flow[a, k, 0])

        def body(i, carry):
            self.add(a, k, i, self.got_c[a][k, i])
            return carry

        lax.fori_loop(0, 4, body, 0)
        self.flow[a, k, 1] = [
            self.sender.go(
                self.spot(a, k, yx, here.c),
                self.got_1[a].at[k, i],
                self.g_sems,
                (a, k, 4 + i),
                here.one,
            )
            for i, yx in ((1, here.yx_12), (0, here.yx_1))
        ]

    def one_take(self, a, k):
        here = self.here
        arrived(self.flow[a, k, 1])
        self.add(a, k, here.yx_2, self.got_1[a][k, 1])
        self.flow[a, k, 2] = [
            self.sender.go(
                self.spot(a, k, here.yx_2, here.c),
                self.got_2[a].at[k],
                self.g_sems,
                (a, k, 6),
                here.two,
            )
        ]
        self.add(a, k, here.yx, self.got_1[a][k, 0])

    def two_take(self, a, k):
        here = self.here
        arrived(self.flow[a, k, 2])
        self.add(a, k, here.yx, self.got_2[a][k])
        spot = self.spot(a, k, here.yx, here.c)
        if k >= 2:
            self.flow[a, k, 3] = [
                self.sender.go(spot, self.got_z[a].at[k - 2], self.g_sems, (a, k, 7), here.far_z)
            ]
        else:
            arrived(self.flow[a, k + 2, 3])
            self.add(a, k, here.yx, self.got_z[a][k])
            if k == 1:
                self.flow[a, k, 3] = [
                    self.sender.go(spot, self.got_z[a].at[2], self.g_sems, (a, k, 7), here.near_z)
                ]

    def z_take(self, a):
        here = self.here
        arrived(self.flow[a, 1, 3])
        self.add(a, 0, here.yx, self.got_z[a][2])
        mine = self.spot(a, 0, here.yx, here.c)
        for i, device in enumerate(here.wide):
            copy = self.sender.go(mine, self.got_w[a].at[i], self.o_sems, (a, 7 + i), device)
            copy.wait_recv()
            copy.wait_send()
            self.sender.started.pop()
            self.add(a, 0, here.yx, self.got_w[a][i])
        r = self.piece(a, here.yx, here.c)
        self.outs[a][r, :] = self.grads[a][here.shard[0], r, :]
        spot = self.outs[a].at[r, :]
        self.flow[a, "o1"] = [self.sender.go(spot, spot, self.o_sems, (a, 0), here.one)]

    def out_two(self, a):
        here = self.here
        arrived(self.flow[a, "o1"])
        out = []
        for i, yx in enumerate((here.yx, here.yx_1)):
            spot = self.outs[a].at[self.piece(a, yx, here.c), :]
            out.append(self.sender.go(spot, spot, self.o_sems, (a, 1 + i), here.two))
        self.flow[a, "o2"] = out

    def out_three(self, a):
        here = self.here
        arrived(self.flow[a, "o2"])
        out = []
        for i in range(4):
            spot = self.outs[a].at[self.piece(a, i, here.c), :]
            out.append(self.sender.go(spot, spot, self.o_sems, (a, 3 + i), here.core))
        self.flow[a, "o3"] = out

    def finish(self, a):
        arrived(self.flow[a, "o3"])


class Totals:
    def __init__(self, here, sender, held, got, sems):
        self.sender, self.held, self.got, self.sems = sender, held, got, sems
        self.ways = [here.core, here.one, here.two, here.near_z, here.far_z, *here.wide]
        self.at = 0

    def start(self):
        i = self.at
        self.copy = self.sender.go(
            self.held.at[i], self.got.at[i], self.sems, (i,), self.ways[i]
        )

    def step(self):
        i = self.at
        self.copy.wait_recv()
        self.held[i + 1] = self.held[i] + self.got[i]
        self.at += 1
        if self.at < len(self.ways):
            self.start()

    def done(self):
        return self.at >= len(self.ways)


def flip(v):
    return jnp.transpose(v)


def mm(a, b):
    return jnp.dot(a, b, preferred_element_type=f32)


def mm_t(a, b):
    return lax.dot_general(a, b, (((1,), (1,)), ((), ())), preferred_element_type=f32)


def attention_forward(s, k, attn, rel, feat, bound, tok_t, q_t, k_t, v_t, probs, att_t, acc, proj):
    part = att_t.shape[1]
    heads = part // HEAD_DIM
    proj[...] = mm(attn[s, 0 : 3 * part, :], tok_t[...]).astype(bf16)
    cos_t, sin_t = feat[0:32, :], feat[32:64, :]
    feat_low = feat[...].astype(bf16)

    def head(h, carry):
        i = k * heads + h
        r0 = pl.multiple_of(h * HEAD_DIM, HEAD_DIM)
        q = proj[pl.ds(r0, HEAD_DIM), :]
        coeffs = lax.dot_general(
            rel[k, pl.ds(r0, HEAD_DIM), :], q, (((0,), (0,)), ((), ())), preferred_element_type=f32
        )
        first, second = coeffs[0:32], coeffs[32:64]
        q_t[i, 0:64, :] = q * score_scale
        q_t[i, 64:96, :] = ((first * sin_t + second * cos_t).astype(bf16)) * score_scale
        q_t[i, 96:128, :] = ((second * sin_t - first * cos_t).astype(bf16)) * score_scale
        k_t[i, 0:64, :] = proj[pl.ds(pl.multiple_of(part + r0, HEAD_DIM), HEAD_DIM), :]
        k_t[i, 64:128, :] = feat_low
        v = proj[pl.ds(pl.multiple_of(2 * part + r0, HEAD_DIM), HEAD_DIM), :]
        v_t[i] = v
        scores = mm(flip(k_t[i]), q_t[i])
        scores = jnp.minimum(scores, jnp.concatenate([bound[...]] * (PAGE // 128), 1))
        top = jnp.max(scores, 0, keepdims=True)
        raised = jnp.exp(scores - top)
        total = jnp.sum(raised, 0, keepdims=True)
        weights = (raised * (1.0 / total)).astype(bf16)
        probs[i] = weights
        att_t[k, pl.ds(r0, HEAD_DIM), :] = mm(v, weights).astype(bf16)
        return carry

    lax.fori_loop(0, heads, head, 0)
    acc[...] += mm(flip(att_t[k]), attn[s, 3 * part : 4 * part, :])


def norm_rows(r, gain, shift):
    average = jnp.mean(r, -1, keepdims=True)
    centred = r - average
    spread = jnp.mean(centred * centred, -1, keepdims=True)
    rstd = lax.rsqrt(spread + norm_epsilon)
    hat = centred * rstd
    return hat, rstd, hat * gain + shift


def norm_rows_back(g, hat, rstd, gain):
    gh = g * gain
    a = jnp.mean(gh, -1, keepdims=True)
    b = jnp.mean(gh * hat, -1, keepdims=True)
    return rstd * (gh - a - hat * b)


def first_norm(tok, acc, hat_one, rstd_one, gains, shifts, live, low, vec):
    vec[8] = jnp.zeros_like(vec[8])
    vec[9] = jnp.zeros_like(vec[9])

    def step(i, carry):
        r = pl.ds(pl.multiple_of(i * ROWS_STEP, ROWS_STEP), ROWS_STEP)
        x = tok[r, :].astype(f32)
        a = acc[r, :]
        hat, rstd, y = norm_rows(x + a, gains[0:1, :], shifts[0:1, :])
        hat_one[r, :] = hat
        rstd_one[r, :] = jnp.broadcast_to(rstd, (ROWS_STEP, 128))
        low[r, :] = y.astype(bf16)
        m = live[r, 0:1]
        vec[8] += jnp.sum(m * x * x, 0, keepdims=True)
        vec[9] += jnp.sum(m * a * a, 0, keepdims=True)
        acc[r, :] = jnp.zeros_like(a)
        return carry

    lax.fori_loop(0, PAGE // ROWS_STEP, step, 0)


def second_norm(acc, hat_one, gains, shifts, live, og, layer_out, grad_low, vec):
    vec[10] = jnp.zeros_like(vec[10])
    vec[1] = jnp.zeros_like(vec[1])
    vec[3] = jnp.zeros_like(vec[3])

    def step(i, carry):
        r = pl.ds(pl.multiple_of(i * ROWS_STEP, ROWS_STEP), ROWS_STEP)
        f = acc[r, :]
        y = hat_one[r, :] * gains[0:1, :] + shifts[0:1, :]
        hat, rstd, out = norm_rows(y + f, gains[1:2, :], shifts[1:2, :])
        layer_out[r, :] = out.astype(bf16)
        m = live[r, 0:1]
        vec[10] += jnp.sum(m * f * f, 0, keepdims=True)
        g = og[r, :].astype(f32)
        vec[1] += jnp.sum(g * hat, 0, keepdims=True)
        vec[3] += jnp.sum(g, 0, keepdims=True)
        back = norm_rows_back(g, hat, rstd, gains[1:2, :])
        acc[r, :] = back
        grad_low[r, :] = back.astype(bf16)
        return carry

    lax.fori_loop(0, PAGE // ROWS_STEP, step, 0)


def first_norm_back(acc, hat_one, rstd_one, gains, grad_low, vec):
    vec[0] = jnp.zeros_like(vec[0])
    vec[2] = jnp.zeros_like(vec[2])

    def step(i, carry):
        r = pl.ds(pl.multiple_of(i * ROWS_STEP, ROWS_STEP), ROWS_STEP)
        g = acc[r, :]
        hat = hat_one[r, :]
        vec[0] += jnp.sum(g * hat, 0, keepdims=True)
        vec[2] += jnp.sum(g, 0, keepdims=True)
        back = norm_rows_back(g, hat, rstd_one[r, 0:1], gains[0:1, :])
        acc[r, :] = back
        grad_low[r, :] = back.astype(bf16)
        return carry

    lax.fori_loop(0, PAGE // ROWS_STEP, step, 0)


def ffn_forward(s, k, w_in, w_out, bias, low, hid_t, slope, hid, acc):
    width = w_in.shape[1]

    def step(j, carry):
        c0 = pl.multiple_of(j * FF_STEP, FF_STEP)
        cols = pl.ds(c0, FF_STEP)
        pre = mm(low[...], w_in[s, :, cols]) + bias[s, :, cols]
        cdf = 0.5 * lax.erf(pre * (2.0**-0.5)) + 0.5
        density = jnp.exp(pre * pre * -0.5) * (1.0 / math.sqrt(2.0 * math.pi))
        slope[k, :, cols] = (cdf + pre * density).astype(bf16)
        act = (pre * cdf).astype(bf16)
        hid[:, cols] = act
        hid_t[k, cols, :] = flip(act)
        return carry

    lax.fori_loop(0, width // FF_STEP, step, 0)
    acc[...] += mm(hid[...], w_out[s])


def ffn_backward(s, k, w_in, w_out, low_t, hid_t, slope, hid, grad_low, acc, vec):
    width = w_in.shape[1]

    def step(j, carry):
        c0 = pl.multiple_of(j * FF_STEP, FF_STEP)
        cols = pl.ds(c0, FF_STEP)
        grad = mm_t(grad_low[...], w_out[s, cols, :])
        pre = (grad * slope[k, :, cols].astype(f32)).astype(bf16)
        hid[:, cols] = pre
        vec[4 + s, :, cols] = jnp.sum(pre.astype(f32), 0, keepdims=True)
        w_out[s, cols, :] = mm(hid_t[k, cols, :], grad_low[...]).astype(bf16)
        return carry

    lax.fori_loop(0, width // FF_STEP, step, 0)
    acc[...] += mm_t(hid[...], w_in[s])
    w_in[s] = mm(low_t[...], hid[...]).astype(bf16)


def attention_backward(s, k, attn, rel, feat, tok, grad_low, grad_low_t, q_t, k_t, v_t, probs, att_t, acc, proj, rel_grad, d_att):
    part = att_t.shape[1]
    heads = part // HEAD_DIM
    d_att[...] = mm(attn[s, 3 * part : 4 * part, :], grad_low_t[...]).astype(bf16)
    attn[s, 3 * part : 4 * part, :] = mm(att_t[k], grad_low[...]).astype(bf16)
    cos_t, sin_t = feat[0:32, :], feat[32:64, :]
    lane = lax.broadcasted_iota(jnp.int32, (HEAD_DIM, 256), 1)
    rel_grad[s] = jnp.zeros((HEAD_DIM, 256), f32)

    def head(h, carry):
        i = k * heads + h
        r0 = pl.multiple_of(h * HEAD_DIM, HEAD_DIM)
        d_out = d_att[pl.ds(r0, HEAD_DIM), :]
        inner = jnp.sum(
            d_out.astype(f32) * att_t[k, pl.ds(r0, HEAD_DIM), :].astype(f32), 0, keepdims=True
        )
        weights = probs[i]
        d_probs = mm(flip(v_t[i]), d_out)
        d_scores = (weights.astype(f32) * (d_probs - inner)).astype(bf16)
        proj[pl.ds(pl.multiple_of(2 * part + r0, HEAD_DIM), HEAD_DIM), :] = mm_t(
            d_out, weights
        ).astype(bf16)
        q_part = q_t[i, 0:64, :]
        proj[pl.ds(pl.multiple_of(part + r0, HEAD_DIM), HEAD_DIM), :] = mm_t(
            q_part, d_scores
        ).astype(bf16)
        d_query = mm(k_t[i], d_scores) * score_scale
        d_turned = d_query[64:128].astype(bf16).astype(f32)
        first, second = d_turned[0:32], d_turned[32:64]
        d_coeffs = jnp.concatenate(
            [first * sin_t - second * cos_t, first * cos_t + second * sin_t], 0
        ).astype(bf16)
        rel_h = rel[k, pl.ds(r0, HEAD_DIM), :]
        proj[pl.ds(r0, HEAD_DIM), :] = (d_query[0:64] + mm(rel_h, d_coeffs)).astype(bf16)
        piece = mm_t(d_coeffs, q_part) * (1.0 / score_scale)
        wide = jnp.concatenate([piece] * 4, 1)
        rel_grad[s] += jnp.where(lane // POS == h, wide, 0.0)
        return carry

    lax.fori_loop(0, heads, head, 0)
    acc[...] += mm(flip(proj[...]), attn[s, 0 : 3 * part, :])
    attn[s, 0 : 3 * part, :] = mm(proj[...], tok[...]).astype(bf16)


def layer_kernel(dp_size, n_wide, *refs):
    it = iter(refs)
    take = lambda n: [next(it) for _ in range(n)]
    tok, qkv_own, rel_own, wo_own, in_own, bias_own, out_own = take(7)
    gains, shifts, lengths, boxes, og = take(5)
    layer_out, tokens_grad = take(2)
    sums = take(4)
    gains_out, shifts_out, bias_out, rms_out = take(4)
    attn, w_in, w_out, rel_t, bias, rel = take(6)
    tok_t, low, low_t, grad_low, grad_low_t = take(5)
    q_t, k_t, v_t, probs, att_t, d_att, proj = take(7)
    acc, hat_one, rstd_one, hid_t, slope, hid, feat, bound, live = take(9)
    rel_grad = next(it)
    got = [take(4) for _ in range(5)]
    held, held_got = take(2)
    local_sem, z_s, z_r, p_s, p_r, m_s, m_r, g_s, g_r, o_s, o_r, t_s, t_r = take(13)

    here = Place(dp_size)
    t = here.t
    shard = here.shard
    part = att_t.shape[1]
    local = [
        pltpu.make_async_copy(source, target, local_sem.at[i])
        for i, (source, target) in enumerate(
            (
                (qkv_own, attn.at[t, 0 : 3 * part, :]),
                (wo_own, attn.at[t, 3 * part : 4 * part, :]),
                (rel_own, rel_t.at[t]),
                (bias_own, bias.at[t]),
                (in_own, w_in.at[t]),
                (out_own, w_out.at[t]),
            )
        )
    ]
    for copy in local:
        copy.start()
    here.meet()
    sender = Sender()
    whole = (attn, w_in, w_out)
    gather = Gather(here, sender, whole, ((z_s, z_r), (p_s, p_r)), attn.shape[1] // SPLIT)
    small = []
    for copy in local[0:4]:
        copy.wait()
    gather.z_start(0)
    for i, every in enumerate((rel_t, bias)):
        spot = every.at[t]
        small.append([sender.go(spot, spot, (m_s, m_r), (i, 0), here.near_z)])
        small[i].append(sender.go(spot, spot, (m_s, m_r), (i, 1), here.far_z))

    tok_t[...] = flip(tok[...])
    acc[...] = jnp.zeros_like(acc)
    page = boxes[:, pl.ds(pl.multiple_of(t * PAGE, PAGE), PAGE)].astype(f32)
    orders = lax.broadcasted_iota(jnp.int32, (FREQ, PAGE), 0).astype(f32)
    rates = 0.5 * jnp.exp(orders * (-math.log(100.0) / FREQ))
    for axis in range(2):
        angles = page[axis : axis + 1, :] * rates
        feat[axis * FREQ : (axis + 1) * FREQ, :] = jnp.cos(angles)
        feat[(axis + 2) * FREQ : (axis + 3) * FREQ, :] = jnp.sin(angles)
    real = lax.broadcasted_iota(jnp.int32, (PAGE, 128), 0) < lengths[t]
    bound[...] = jnp.where(real, 3e38, masked_score)
    live[...] = jnp.where(real, 1.0, 0.0)
    vec = held.at[0]

    gather.z_relay(0)
    for i, every in enumerate((rel_t, bias)):
        arrived(small[i][0:1])
        spot = every.at[shard[1]]
        small[i].append(sender.go(spot, spot, (m_s, m_r), (i, 2), here.far_z))
    for copy in local[4:6]:
        copy.wait()
    gather.z_start(1)

    def attend(k):
        if k > 1:
            arrived(small[0][k - 1 : k])
        rel[k] = flip(rel_t[shard[k]])
        attention_forward(
            shard[k], k, attn, rel, feat, bound, tok_t, q_t, k_t, v_t, probs, att_t, acc, proj
        )

    def feed(k):
        if k > 1:
            arrived(small[1][k - 1 : k])
        ffn_forward(shard[k], k, w_in, w_out, bias, low, hid_t, slope, hid, acc)

    gather.one(0, 1)
    attend(0)
    gather.one(0, 2)
    gather.two(0, 1)
    gather.z_relay(1)
    gather.z_start(2)
    gather.one(1, 1)
    gather.one(0, 3)
    gather.two(0, 2)
    gather.three(0, 1)
    gather.two(0, 3)
    gather.ready(0, 1)
    attend(1)
    gather.two(1, 1)
    gather.three(0, 2)
    gather.one(1, 2)
    gather.ready(0, 2)
    gather.z_relay(2)
    gather.one(2, 1)
    gather.three(0, 3)
    attend(2)
    gather.three(1, 1)
    gather.two(1, 2)
    gather.one(1, 3)
    gather.two(2, 1)
    gather.ready(0, 3)
    attend(3)
    gather.three(1, 2)
    gather.three(2, 1)
    gather.two(1, 3)
    gather.one(2, 2)
    first_norm(tok, acc, hat_one, rstd_one, gains, shifts, live, low, vec)
    feed(0)
    gather.ready(1, 1)
    gather.ready(2, 1)
    gather.two(2, 2)
    gather.one(2, 3)
    gather.three(1, 3)
    low_t[...] = flip(low[...])
    feed(1)
    gather.two(2, 3)
    gather.three(2, 2)
    gather.ready(1, 2)
    gather.ready(2, 2)
    feed(2)
    gather.three(2, 3)
    gather.ready(1, 3)
    gather.ready(2, 3)
    feed(3)
    sender.drain()

    second_norm(acc, hat_one, gains, shifts, live, og, layer_out, grad_low, vec)

    grads = (attn, w_in, w_out, rel_grad)
    rows = [g.shape[1] // SPLIT for g in grads]
    reduce = Reduce(here, sender, grads, sums, got, ((g_s, g_r), (o_s, o_r)), rows)
    totals = Totals(here, sender, held, held_got, (t_s, t_r))

    def feed_back(k):
        ffn_backward(
            shard[k], k, w_in, w_out, low_t, hid_t, slope, hid, grad_low, acc, vec
        )
        reduce.c_send(1, k)
        reduce.c_send(2, k)

    def attend_back(k):
        attention_backward(
            shard[k],
            k,
            attn,
            rel,
            feat,
            tok,
            grad_low,
            grad_low_t,
            q_t,
            k_t,
            v_t,
            probs,
            att_t,
            acc,
            proj,
            rel_grad,
            d_att,
        )
        reduce.c_send(0, k)
        reduce.c_send(3, k)

    def pair(step, k):
        step(1, k)
        step(2, k)

    def heads(step, k):
        step(0, k)
        step(3, k)

    feed_back(3)
    feed_back(2)
    pair(reduce.c_take, 3)
    feed_back(1)
    pair(reduce.c_take, 2)
    pair(reduce.one_take, 3)
    feed_back(0)
    pair(reduce.c_take, 1)
    first_norm_back(acc, hat_one, rstd_one, gains, grad_low, vec)
    grad_low_t[...] = flip(grad_low[...])
    vec[11] = jnp.broadcast_to(jnp.sum(live[:, 0:1], 0, keepdims=True), (1, vec.shape[2]))
    totals.start()
    pair(reduce.two_take, 3)
    pair(reduce.one_take, 2)
    pair(reduce.c_take, 0)
    attend_back(3)
    totals.step()
    pair(reduce.one_take, 1)
    pair(reduce.two_take, 2)
    heads(reduce.c_take, 3)
    attend_back(2)
    totals.step()
    pair(reduce.one_take, 0)
    pair(reduce.two_take, 1)
    heads(reduce.c_take, 2)
    attend_back(1)
    totals.step()
    heads(reduce.one_take, 3)
    pair(reduce.two_take, 0)
    heads(reduce.c_take, 1)
    attend_back(0)
    tokens_grad[...] = acc[...].astype(bf16)
    totals.step()
    reduce.z_take(1)
    reduce.z_take(2)
    heads(reduce.one_take, 2)
    heads(reduce.two_take, 3)
    heads(reduce.c_take, 0)
    totals.step()
    reduce.out_two(1)
    reduce.out_two(2)
    heads(reduce.one_take, 1)
    heads(reduce.two_take, 2)
    reduce.out_three(1)
    reduce.out_three(2)
    heads(reduce.one_take, 0)
    heads(reduce.two_take, 1)
    heads(reduce.two_take, 0)
    heads(lambda a, k: reduce.z_take(a), 0)
    while not totals.done():
        totals.step()
    final = held.at[totals.at]
    for i in range(2):
        gains_out[i : i + 1, :] = final[i]
        shifts_out[i : i + 1, :] = final[2 + i]
    bias_out[...] = final[4 + t]
    count = final[11] * float(gains.shape[1])
    lane = lax.broadcasted_iota(jnp.int32, (1, 128), 1)
    roots = jnp.zeros((1, 128), f32)
    for i in range(3):
        square = jnp.sum(final[8 + i], 1, keepdims=True)
        roots = roots + jnp.where(lane == i, jnp.sqrt(square / count[:, 0:1]), 0.0)
    rms_out[...] = roots
    heads(lambda a, k: reduce.out_two(a), 0)
    reduce.finish(1)
    reduce.finish(2)
    heads(lambda a, k: reduce.out_three(a), 0)
    heads(lambda a, k: reduce.finish(a), 0)
    sender.drain()


def run_layer(dp_size, arrays):
    tok, qkv, rel, wo, w_in, bias, w_out, gains, shifts, lengths, boxes, og = arrays
    rows, width = tok.shape
    part = wo.shape[0]
    units = w_in.shape[1]
    shards = lengths.shape[0]
    heads = shards * (part // HEAD_DIM)
    n_wide = max(0, (dp_size // SPLIT).bit_length() - 1)
    steps = 5 + n_wide
    piece = 4 * part // SPLIT
    vmem = pl.BlockSpec(memory_space=pltpu.VMEM)
    smem = pl.BlockSpec(memory_space=pltpu.SMEM)
    anywhere = pl.BlockSpec(memory_space=pl.ANY)
    dma = pltpu.SemaphoreType.DMA
    V = pltpu.VMEM
    S = jax.ShapeDtypeStruct
    scratch = [
        V((shards, 4 * part, width), bf16),
        V((shards, width, units), bf16),
        V((shards, units, width), bf16),
        V((shards,) + rel.shape, bf16),
        V((shards, 1, units), f32),
        V((shards, part, POS), bf16),
        V((width, rows), bf16),
        V((rows, width), bf16),
        V((width, rows), bf16),
        V((rows, width), bf16),
        V((width, rows), bf16),
        V((heads, HEAD_DIM + POS, rows), bf16),
        V((heads, HEAD_DIM + POS, rows), bf16),
        V((heads, HEAD_DIM, rows), bf16),
        V((heads, rows, rows), bf16),
        V((shards, part, rows), bf16),
        V((part, rows), bf16),
        V((3 * part, rows), bf16),
        V((rows, width), f32),
        V((rows, width), f32),
        V((rows, 128), f32),
        V((shards, units, rows), bf16),
        V((shards, rows, units), bf16),
        V((rows, units), bf16),
        V((POS, rows), f32),
        V((rows, 128), f32),
        V((rows, 128), f32),
        V((shards, POS, REL_LANES), f32),
    ]
    forms = [
        (4 * part // SPLIT, width, bf16),
        (width // SPLIT, units, bf16),
        (units // SPLIT, width, bf16),
        (POS // SPLIT, REL_LANES, f32),
    ]
    for lead in ((4, 4), (4, 2), (4,), (3,), (max(1, n_wide),)):
        scratch += [V(lead + (a, b), kind) for a, b, kind in forms]
    scratch += [V((steps + 1, 12, 1, width), f32), V((steps, 12, 1, width), f32)]
    scratch += [dma((6,))]
    scratch += [dma((3, 3))] * 2
    scratch += [dma((3, 4, 7))] * 2
    scratch += [dma((2, 3))] * 2
    scratch += [dma((4, 4, 8))] * 2
    scratch += [dma((4, 7 + max(1, n_wide)))] * 2
    scratch += [dma((steps,))] * 2
    shapes = [S((rows, width), bf16), S((rows, width), bf16)]
    shapes += [S((SPLIT * a, b), kind) for a, b, kind in forms]
    shapes += [S((2, width), f32), S((2, width), f32), S((1, units), f32), S((1, 128), f32)]
    return pl.pallas_call(
        partial(layer_kernel, dp_size, n_wide),
        out_shape=shapes,
        in_specs=[vmem] + [anywhere] * 6 + [vmem, vmem, smem, vmem, vmem],
        out_specs=[vmem] * len(shapes),
        scratch_shapes=scratch,
        compiler_params=pltpu.CompilerParams(
            collective_id=0, has_side_effects=True, vmem_limit_bytes=67043328
        ),
        name="layer",
    )(*arrays)


def per_device(
    dp_size,
    tokens,
    qkv_weight,
    rel_weight,
    out_weight,
    ffn_in_weight,
    ffn_in_bias,
    ffn_out_weight,
    norm_gains,
    norm_biases,
    page_lengths,
    boxes,
    out_grad,
):
    width = tokens.shape[1]
    part = out_weight.shape[0]
    (
        layer_out,
        tokens_grad,
        attn_sum,
        in_sum,
        out_sum,
        rel_sum,
        gains_grad,
        biases_grad,
        bias_grad,
        roots,
    ) = run_layer(
        dp_size,
        (
            tokens,
            jnp.transpose(qkv_weight, (0, 2, 1)).reshape(3 * part, width),
            jnp.transpose(rel_weight),
            out_weight,
            ffn_in_weight,
            ffn_in_bias.reshape(1, -1),
            ffn_out_weight,
            norm_gains,
            norm_biases,
            page_lengths,
            boxes,
            out_grad,
        ),
    )
    return (
        layer_out,
        tokens_grad,
        jnp.transpose(attn_sum[: 3 * part].reshape(3, part, width), (0, 2, 1)).astype(f32),
        jnp.transpose(rel_sum[:, :part]),
        attn_sum[3 * part :].astype(f32),
        in_sum.astype(f32),
        bias_grad.reshape(-1),
        out_sum.astype(f32),
        gains_grad,
        biases_grad,
        roots[0, :3],
    )


def solution(mesh):
    return jax.shard_map(
        partial(per_device, mesh.shape["dp"]),
        mesh=mesh,
        in_specs=(
            P(("dp", "tensor"), None),
            P(None, None, "tensor"),
            P("tensor", None),
            P("tensor", None),
            P(None, "tensor"),
            P("tensor"),
            P("tensor", None),
            P(),
            P(),
            P("dp"),
            P(None, "dp"),
            P(("dp", "tensor"), None),
        ),
        out_specs=(
            P(("dp", "tensor"), None),
            P(("dp", "tensor"), None),
            P(None, None, "tensor"),
            P("tensor", None),
            P("tensor", None),
            P(None, "tensor"),
            P("tensor"),
            P("tensor", None),
            P(),
            P(),
            P(),
        ),
        check_vma=False,
    )
```
